32 devices in a mesh: ctx: 4 (over y, x), fsdp: 8 (over z, core).
Axes of the slice: x: 2, y: 2, z: 4, core: 2. Of those that a mesh axis runs over, the one named last changes fastest.
Arguments:
- inputs: bfloat16 [8, 1024, 2560], P('fsdp', 'ctx'), may hold values from -6 to 6
- attn_norm: bfloat16 [2560], P('fsdp'), may hold values from 0.099609375 to 1.8984375
- query_key_value_weight: bfloat16 [2560, 3840], P('fsdp'), may hold values from -0.125 to 0.125
- w_out: bfloat16 [2560, 2560], P('fsdp'), may hold values from -1 to 1
- mlp_norm: bfloat16 [2560], P('fsdp'), may hold values from 0.099609375 to 1.8984375
- w_gate: bfloat16 [2560, 6912], P('fsdp'), may hold values from -0.125 to 0.125
- w_up: bfloat16 [2560, 6912], P('fsdp'), may hold values from -0.125 to 0.125
- w_down: bfloat16 [6912, 2560], P('fsdp'), may hold values from -0.078125 to 0.078125
- cotangent: bfloat16 [8, 1024, 2560], P('fsdp', 'ctx'), may hold values from -6 to 6
- lengths: int32 [8, 4], P('fsdp'), may hold values from 1 to 512, 1024 in all within a row
- block_perm: int32 [8, 8], P('fsdp'), may hold values from 0 to 7, each once within a row
Outputs:
- output: float32 [8, 1024, 2560], P('fsdp', 'ctx')
- grad_inputs: float32 [8, 1024, 2560], P('fsdp', 'ctx')
- grad_attn_norm: float32 [2560], P('fsdp')
- grad_w_qkv: float32 [2560, 3840], P('fsdp')
- grad_w_out: float32 [2560, 2560], P('fsdp')
- grad_mlp_norm: float32 [2560], P('fsdp')
- grad_w_gate: float32 [2560, 6912], P('fsdp')
- grad_w_up: float32 [2560, 6912], P('fsdp')
- grad_w_down: float32 [6912, 2560], P('fsdp')
The draws below stay inside these ranges and needn't reach their ends.
Inputs may be any that keep to these rules, and one draw needn't show every extreme that they name: Each row lists the lengths of 3 sequences packed in order from a group's first place, then the count of padding places at its end; a row sums to 1024 and its largest entry is 512. `block_perm`: each row is a permutation of 0 to 7.
All inputs are finite; a program needn't handle non-finite values.
Results may differ from the reference program's by a relative error of at most 0.019.
Values may be sent and summed in bfloat16 or wider, within the bound.
No kernel may reach another device: no remote copies, remote signals or barrier semaphores. Data moves between devices by JAX's collectives and lax.ppermute only.
A program may use at most 768 MiB of HBM per device.

```python
import math
import jax
import jax.numpy as jnp
import numpy as np
from jax import lax

MODEL_WIDTH = 2560
FF = 6912
QUERY_HEADS = 32
KEY_VALUE_HEADS = 8
HEAD_SIZE = 80
WINDOW = 4096
BLOCK = 128
SEQS = 3
GROUP_TOK = 1024
SEQ_MOST = 512
NBLK = 8
GROUPS = 8


def level_of(own_key, extent, cuts, smallest, top_value):
    def one(dim, blocks):
        draws = jax.random.uniform(jax.random.fold_in(jax.random.fold_in(own_key, 6), dim), (blocks,), jnp.float32, smallest / len(cuts), top_value / len(cuts))
        return jnp.repeat(jnp.exp(draws), extent[dim] // blocks).reshape((-1,) + (1,) * (len(extent) - dim - 1))

    gain = one(*cuts[0])
    for cut in cuts[1:]:
        gain = gain * one(*cut)
    return gain


def length_profile(count, total, limit, skew):
    loads = [(1 << 20) // math.isqrt(rank ** skew) + 1 for rank in range(2, count + 1)]
    spare, holding = total - limit - (count - 1), [1] * (count - 1)
    while spare > 0:
        movable = [i for i in range(count - 1) if holding[i] < limit]
        pool, budget = sum([loads[i] for i in movable]), spare
        for i in movable:
            more = min(limit - holding[i], max(1, budget * loads[i] // pool), spare)
            holding[i] = holding[i] + more
            spare = spare - more
    return np.array([limit] + holding)


def uneven(key, amount, total, reach, skew):
    if amount == 2:
        one = jax.random.randint(key, (), max(1, total - reach), min(reach, total - 1) + 1)
        return jnp.stack([one, total - one])
    sizes = jnp.asarray(length_profile(amount, total, reach, skew), jnp.int32)
    pairs = (amount - 1) // 2
    donor, sink = sizes[1:1 + 2 * pairs:2], sizes[2:2 + 2 * pairs:2]
    margin = jnp.minimum(donor - 1, reach - sink)
    moved = jax.random.randint(jax.random.fold_in(key, 1), (pairs,), 0, 1 << 20) % (margin + 1)
    sizes = sizes.at[1:1 + 2 * pairs:2].set(donor - moved).at[2:2 + 2 * pairs:2].set(sink + moved)
    return sizes[jax.random.permutation(jax.random.fold_in(key, 2), amount)]


def noise(key, extent, scale, most, shards=(), kind=jnp.bfloat16):
    values = scale * jax.random.normal(key, extent, jnp.float32)
    if shards:
        values = values * level_of(key, extent, shards, -0.22, 0.18)
    return jnp.clip(values, -most, most).astype(kind)


def setup_inputs(seed: int = 0) -> dict:
    key_of = jax.random.split(jax.random.key(seed), 12)
    return {
        "inputs": noise(key_of[0], (GROUPS, GROUP_TOK, MODEL_WIDTH), 1.0, 6.0, ((0, 8), (1, 4))),
        "attn_norm": jnp.clip(1.0 + 0.18 * jax.random.normal(key_of[1], (MODEL_WIDTH,), jnp.float32), 0.099609375, 1.8984375).astype(jnp.bfloat16),
        "query_key_value_weight": noise(key_of[2], (MODEL_WIDTH, (QUERY_HEADS + 2 * KEY_VALUE_HEADS) * HEAD_SIZE), MODEL_WIDTH ** -0.5, 0.125, ((0, 8),)),
        "w_out": noise(key_of[3], (QUERY_HEADS * HEAD_SIZE, MODEL_WIDTH), (max(QUERY_HEADS * HEAD_SIZE // 64, 4)) ** -0.5, 1.0, ((0, 8),)),
        "mlp_norm": jnp.clip(1.0 + 0.18 * jax.random.normal(key_of[4], (MODEL_WIDTH,), jnp.float32), 0.099609375, 1.8984375).astype(jnp.bfloat16),
        "w_gate": noise(key_of[5], (MODEL_WIDTH, FF), MODEL_WIDTH ** -0.5, 0.125, ((0, 8),)),
        "w_up": noise(key_of[6], (MODEL_WIDTH, FF), MODEL_WIDTH ** -0.5, 0.125, ((0, 8),)),
        "w_down": noise(key_of[7], (FF, MODEL_WIDTH), FF ** -0.5, 0.078125, ((0, 8),)),
        "cotangent": noise(key_of[8], (GROUPS, GROUP_TOK, MODEL_WIDTH), 1.0, 6.0, ((0, 8), (1, 4))),
        "lengths": jax.vmap(lambda own: uneven(own, SEQS + 1, GROUP_TOK, SEQ_MOST, 2))(jax.random.split(key_of[9], GROUPS)).reshape((GROUPS, SEQS + 1)).astype(jnp.int32),
        "block_perm": jax.vmap(lambda own: jax.random.permutation(own, NBLK))(jax.random.split(key_of[10], GROUPS)).reshape((GROUPS, NBLK)).astype(jnp.int32),
    }


EPS = 1e-05
THETA = 10000.0
NEG = -1e+30
HIGH = lax.Precision.HIGHEST

@jax.custom_vjp
def lower_precision(v):
    return lax.optimization_barrier(v.astype(jnp.bfloat16)).astype(jnp.float32)

@jax.custom_vjp
def low_back(v):
    return v

def low_keep(v):
    return (lower_precision(v), None)

def low_pass(kept, grad):
    return (grad,)

def back_keep(v):
    return (v, None)

def back_low(kept, grad):
    return (lower_precision(grad),)
lower_precision.defvjp(low_keep, low_pass)
low_back.defvjp(back_keep, back_low)

def token_places(perm_row, len_row, rows):
    blocks = rows // BLOCK
    onehot = blocks[:, None] == jnp.arange(perm_row.shape[0], dtype=jnp.int32)[None, :]
    place = lax.optimization_barrier(jnp.sum(jnp.where(onehot, perm_row[None, :], 0), axis=1, dtype=jnp.int32)) * BLOCK + rows % BLOCK
    ends = jnp.cumsum(len_row, dtype=jnp.int32)
    segment = lax.optimization_barrier(jnp.sum((place[:, None] >= ends[None, :]).astype(jnp.int32), axis=1, dtype=jnp.int32))
    starts = ends - len_row
    choose = segment[:, None] == jnp.arange(len_row.shape[0], dtype=jnp.int32)[None, :]
    inner = place - lax.optimization_barrier(jnp.sum(jnp.where(choose, starts[None, :], 0), axis=1, dtype=jnp.int32))
    return (place, segment, inner)

def visible(q_place, q_seg, q_rows, k_place, k_seg, k_rows, num_seqs):
    same = (q_seg[:, None] == k_seg[None, :]) & (q_seg[:, None] < num_seqs)
    causal = (k_place[None, :] <= q_place[:, None]) & (q_place[:, None] - k_place[None, :] < WINDOW)
    return same & causal | (q_rows[:, None] == k_rows[None, :])

def rope_tables(inner):
    half = HEAD_SIZE // 2
    freq = THETA ** (-(jnp.arange(half, dtype=jnp.float32) * 2.0 / HEAD_SIZE))
    angle = inner.astype(jnp.float32)[:, None] * freq[None, :]
    return (jnp.cos(angle)[:, None, :], jnp.sin(angle)[:, None, :])

def apply_rotary(value_vectors, cosine_table, sine_table):
    half = value_vectors.shape[-1] // 2
    first, second = (value_vectors[..., :half], value_vectors[..., half:])
    return jnp.concatenate([first * cosine_table - second * sine_table, second * cosine_table + first * sine_table], axis=-1)

def rms(value_vectors):
    return value_vectors * lax.rsqrt(lax.optimization_barrier(jnp.mean(value_vectors * value_vectors, axis=-1, keepdims=True)) + EPS)

def layer(weights, tokens, allowed, cosine_table, sine_table):
    gain_one, weight_qkv, weight_out, gain_two, weight_gate, weight_up, weight_down = weights
    head_group = tokens.shape[0]
    query_total_width = QUERY_HEADS * HEAD_SIZE
    key_value_width = KEY_VALUE_HEADS * HEAD_SIZE
    queries_per_group = QUERY_HEADS // KEY_VALUE_HEADS
    scaling = HEAD_SIZE ** (-0.5)
    hidden_one = lower_precision(rms(tokens) * gain_one)
    projected_rows = low_back(jnp.dot(hidden_one, weight_qkv, precision=HIGH))
    query_vectors = lower_precision(apply_rotary(projected_rows[:, :query_total_width].reshape(head_group, QUERY_HEADS, HEAD_SIZE), cosine_table, sine_table))
    key_vectors = lower_precision(apply_rotary(projected_rows[:, query_total_width:query_total_width + key_value_width].reshape(head_group, KEY_VALUE_HEADS, HEAD_SIZE), cosine_table, sine_table))
    value_vectors = lower_precision(projected_rows[:, query_total_width + key_value_width:].reshape(head_group, KEY_VALUE_HEADS, HEAD_SIZE))
    query_heads = query_vectors.reshape(head_group, KEY_VALUE_HEADS, queries_per_group, HEAD_SIZE).transpose(1, 2, 0, 3)

    def head_fn(items):
        query_h, key_h, value_h = items
        scores = low_back(jnp.einsum('gtd,kd->gtk', query_h, key_h, precision=HIGH)) * scaling
        scores = jnp.where(allowed[None], scores, NEG)
        peak = lax.optimization_barrier(jnp.max(scores, axis=-1, keepdims=True))
        raised = jnp.exp(scores - peak)
        probs = raised / lax.optimization_barrier(jnp.sum(raised, axis=-1, keepdims=True))
        return jnp.einsum('gtk,kd->gtd', lower_precision(probs), value_h, precision=HIGH)
    attended = lax.map(jax.checkpoint(head_fn), (query_heads, key_vectors.transpose(1, 0, 2), value_vectors.transpose(1, 0, 2)))
    merged = attended.transpose(2, 0, 1, 3).reshape(head_group, query_total_width)
    merged = lower_precision(low_back(merged))
    middle = tokens + low_back(jnp.dot(merged, weight_out, precision=HIGH))
    hidden_two = lower_precision(rms(middle) * gain_two)
    gate = low_back(jnp.dot(hidden_two, weight_gate, precision=HIGH))
    upper = low_back(jnp.dot(hidden_two, weight_up, precision=HIGH))
    activated = lower_precision(jax.nn.silu(gate) * upper)
    return middle + low_back(jnp.dot(activated, weight_down, precision=HIGH))

def reference(inputs, attn_norm, query_key_value_weight, w_out, mlp_norm, w_gate, w_up, w_down, cotangent, lengths, block_perm):
    params = (attn_norm.astype(jnp.float32), query_key_value_weight.astype(jnp.float32), w_out.astype(jnp.float32), mlp_norm.astype(jnp.float32), w_gate.astype(jnp.float32), w_up.astype(jnp.float32), w_down.astype(jnp.float32))
    head_group = inputs.shape[1]
    key_rows = jnp.arange(head_group, dtype=jnp.int32)

    def one_group(carry, items):
        tokens_in, cot_in, len_row, perm_row = items
        place, segment, inner = token_places(perm_row, len_row, key_rows)
        allowed = visible(place, segment, key_rows, place, segment, key_rows, len_row.shape[0] - 1)
        cosine_table, sine_table = rope_tables(inner)

        def forward(weights, tokens):
            return layer(weights, tokens, allowed, cosine_table, sine_table)
        result, pullback = jax.vjp(forward, params, tokens_in)
        grads, grad_in = pullback(cot_in)
        carry = jax.tree.map(lambda summed, fresh: summed + fresh, carry, grads)
        return (carry, (result, grad_in))
    zeros = tuple((jnp.zeros_like(weight) for weight in params))
    totals, stacked = lax.scan(one_group, zeros, (inputs.astype(jnp.float32), cotangent.astype(jnp.float32), lengths, block_perm))
    return (stacked[0], stacked[1], totals[0], totals[1], totals[2], totals[3], totals[4], totals[5], totals[6])
```

```python
import functools

import jax
import jax.numpy as jnp
from jax import lax
from jax.experimental import pallas as pl
from jax.experimental.pallas import tpu as pltpu
from jax.sharding import PartitionSpec as P

QUERY_HEADS = 32
KEY_VALUE_HEADS = 8
HEAD_SIZE = 80
WINDOW = 4096
BLOCK = 128

EPS = 1e-05
THETA = 10000.0
NEG = -1e30
CHUNK = 256


F32 = jnp.float32
BF16 = jnp.bfloat16


def token_places(perm_row, len_row, rows):
    blocks = rows // BLOCK
    onehot = blocks[:, None] == jnp.arange(perm_row.shape[0], dtype=jnp.int32)[None, :]
    place = (
        jnp.sum(jnp.where(onehot, perm_row[None, :], 0), axis=1, dtype=jnp.int32) * BLOCK
        + rows % BLOCK
    )
    ends = jnp.cumsum(len_row, dtype=jnp.int32)
    segment = jnp.sum((place[:, None] >= ends[None, :]).astype(jnp.int32), axis=1, dtype=jnp.int32)
    starts = ends - len_row
    choose = segment[:, None] == jnp.arange(len_row.shape[0], dtype=jnp.int32)[None, :]
    inner = place - jnp.sum(jnp.where(choose, starts[None, :], 0), axis=1, dtype=jnp.int32)
    return (place, segment, inner)


def mask_bias(place, seg, rows, num_seqs):
    same = (seg[:, None] == seg[None, :]) & (seg[None, :] < num_seqs)
    ahead = place[None, :] - place[:, None]
    allowed = same & (ahead >= 0) & (ahead < WINDOW) | (rows[:, None] == rows[None, :])
    return jnp.where(allowed, 0.0, NEG).astype(F32)


def rope_tables(inner):
    half = HEAD_SIZE // 2
    freq = THETA ** (-(jnp.arange(half, dtype=F32) * 2.0 / HEAD_SIZE))
    angle = freq[:, None] * inner.astype(F32)[None, :]
    return (jnp.cos(angle), jnp.sin(angle))


def rotate(heads, cosine, sine):
    half = HEAD_SIZE // 2
    first, second = heads[:, :half], heads[:, half:]
    return jnp.concatenate(
        [first * cosine - second * sine, second * cosine + first * sine], axis=1
    )


def rms_scale(v):
    return lax.rsqrt(jnp.mean(v * v, axis=-1, keepdims=True) + EPS)


def rms_back(normed, factor, grads):
    return factor * (grads - normed * jnp.mean(grads * normed, axis=-1, keepdims=True))


def matmul(a, b, ca, cb):
    return lax.dot_general(a, b, (((ca,), (cb,)), ((), ())), preferred_element_type=F32)


def attend_kernel(q_ref, k_ref, vt_ref, bias_ref, o_ref, lse_ref):
    scaling = HEAD_SIZE ** (-0.5)
    tokens = k_ref.shape[1]
    key = k_ref[0]
    value_t = vt_ref[0]
    for c in range(tokens // CHUNK):
        cols = slice(c * CHUNK, (c + 1) * CHUNK)
        scores = matmul(key, q_ref[0, :, cols], 1, 0) * scaling + bias_ref[:, cols]
        peak = jnp.max(scores, axis=0, keepdims=True)
        raised = jnp.exp(scores - peak)
        total = jnp.sum(raised, axis=0, keepdims=True)
        probs = (raised * (1.0 / total)).astype(BF16)
        o_ref[0, :, cols] = matmul(value_t, probs, 1, 0).astype(BF16)
        lse_ref[0, :, cols] = peak + jnp.log(total)


def attend(q_t, key, v_t, bias):
    heads, size, tokens = q_t.shape
    kv = key.shape[0]
    per = heads // kv
    return pl.pallas_call(
        attend_kernel,
        grid=(kv, per),
        in_specs=[
            pl.BlockSpec((1, size, tokens), lambda i, j: (i * per + j, 0, 0)),
            pl.BlockSpec((1, tokens, size), lambda i, j: (i, 0, 0)),
            pl.BlockSpec((1, size, tokens), lambda i, j: (i, 0, 0)),
            pl.BlockSpec((tokens, tokens), lambda i, j: (0, 0)),
        ],
        out_specs=[
            pl.BlockSpec((1, size, tokens), lambda i, j: (i * per + j, 0, 0)),
            pl.BlockSpec((1, 1, tokens), lambda i, j: (i * per + j, 0, 0)),
        ],
        out_shape=[
            jax.ShapeDtypeStruct((heads, size, tokens), BF16),
            jax.ShapeDtypeStruct((heads, 1, tokens), F32),
        ],
        cost_estimate=pl.CostEstimate(
            flops=4 * heads * tokens * tokens * size,
            bytes_accessed=4 * tokens * tokens + 6 * heads * tokens * size,
            transcendentals=heads * tokens * tokens,
        ),
        name="attend",
    )(q_t, key, v_t, bias)


def attend_back_kernel(
    q_ref, k_ref, kt_ref, v_ref, bias_ref, lse_ref, do_ref, dq_ref, dk_ref, dv_ref
):
    scaling = HEAD_SIZE ** (-0.5)
    tokens = k_ref.shape[1]
    key, key_t, value = k_ref[0], kt_ref[0], v_ref[0]

    @pl.when(pl.program_id(1) == 0)
    def _():
        dk_ref[...] = jnp.zeros_like(dk_ref)
        dv_ref[...] = jnp.zeros_like(dv_ref)

    for c in range(tokens // CHUNK):
        cols = slice(c * CHUNK, (c + 1) * CHUNK)
        q, grad = q_ref[0, :, cols], do_ref[0, :, cols]
        scores = matmul(key, q, 1, 0) * scaling + bias_ref[:, cols]
        probs = jnp.exp(scores - lse_ref[0, :, cols])
        grad_probs = matmul(value, grad, 1, 0)
        inner = jnp.sum(probs * grad_probs, axis=0, keepdims=True)
        grad_scores = (probs * (grad_probs - inner) * scaling).astype(BF16)
        dq_ref[0, :, cols] = matmul(key_t, grad_scores, 1, 0)
        dk_ref[0] += matmul(q, grad_scores, 1, 1)
        dv_ref[0] += matmul(grad, probs.astype(BF16), 1, 1)


def attend_back(q_t, key, k_t, value, bias, lse, do_t):
    heads, size, tokens = q_t.shape
    kv = key.shape[0]
    per = heads // kv
    by_head = lambda i, j: (i * per + j, 0, 0)
    by_kv = lambda i, j: (i, 0, 0)
    return pl.pallas_call(
        attend_back_kernel,
        grid=(kv, per),
        in_specs=[
            pl.BlockSpec((1, size, tokens), by_head),
            pl.BlockSpec((1, tokens, size), by_kv),
            pl.BlockSpec((1, size, tokens), by_kv),
            pl.BlockSpec((1, tokens, size), by_kv),
            pl.BlockSpec((tokens, tokens), lambda i, j: (0, 0)),
            pl.BlockSpec((1, 1, tokens), by_head),
            pl.BlockSpec((1, size, tokens), by_head),
        ],
        out_specs=[
            pl.BlockSpec((1, size, tokens), by_head),
            pl.BlockSpec((1, size, tokens), by_kv),
            pl.BlockSpec((1, size, tokens), by_kv),
        ],
        out_shape=[
            jax.ShapeDtypeStruct((heads, size, tokens), F32),
            jax.ShapeDtypeStruct((kv, size, tokens), F32),
            jax.ShapeDtypeStruct((kv, size, tokens), F32),
        ],
        cost_estimate=pl.CostEstimate(
            flops=10 * heads * tokens * tokens * size,
            bytes_accessed=4 * tokens * tokens + 10 * heads * tokens * size,
            transcendentals=heads * tokens * tokens,
        ),
        name="attend_back",
    )(q_t, key, k_t, value, bias, lse, do_t)


class Comm:
    def __init__(self, ctx_size, fsdp_size):
        self.c, self.f = ctx_size, fsdp_size
        self.me = lax.axis_index("ctx")

    def swap(self, x, j):
        return lax.ppermute(x, "ctx", [(i, i ^ j) for i in range(self.c)])

    def pieces(self, x):
        if self.c == 4:
            half = x.shape[0] // 2
            a, b = self.swap(x, 1), self.swap(x, 2)
            low, high = self.swap(b[:half], 1), self.swap(a[half:], 2)
            return [x, a, b, jnp.concatenate([low, high], axis=0)]
        return [x] + [self.swap(x, j) for j in range(1, self.c)]

    def gather(self, x):
        return jnp.concatenate(self.pieces(x), axis=0)

    def scatter(self, partial):
        rows = partial.shape[0] // self.c
        blocks = [partial[j * rows : (j + 1) * rows] for j in range(self.c)]
        if self.c == 4:
            half = rows // 2
            low = self.swap(blocks[3][:half].astype(BF16), 1).astype(F32)
            high = self.swap(blocks[3][half:].astype(BF16), 2).astype(F32)
            one = jnp.concatenate([blocks[1][:half], blocks[1][half:] + high], axis=0)
            two = jnp.concatenate([blocks[2][:half] + low, blocks[2][half:]], axis=0)
            return (
                blocks[0]
                + self.swap(one.astype(BF16), 1).astype(F32)
                + self.swap(two.astype(BF16), 2).astype(F32)
            )
        total = blocks[0]
        for j in range(1, self.c):
            total = total + self.swap(blocks[j].astype(BF16), j).astype(F32)
        return total

    def absolute(self, pieces):
        stack = jnp.stack(pieces)
        return [
            lax.dynamic_index_in_dim(stack, self.me ^ p, 0, keepdims=False) for p in range(self.c)
        ]

    def deal(self, shard):
        n = shard.shape[0] // self.c
        piece = lax.dynamic_slice_in_dim(shard, self.me * n, n, 0)
        pairs = [(c * self.f + s, s * self.c + c) for c in range(self.c) for s in range(self.f)]
        return lax.ppermute(piece, ("ctx", "fsdp"), pairs)

    def undeal(self, piece):
        pairs = [(s * self.c + c, c * self.f + s) for c in range(self.c) for s in range(self.f)]
        return lax.ppermute(piece, ("ctx", "fsdp"), pairs)

    def columns(self, shard):
        n = shard.shape[1] // self.c
        return lax.dynamic_slice_in_dim(shard, self.me * n, n, 1)

    def weight(self, x):
        return lax.all_gather(x, "fsdp", axis=0, tiled=True)

    def grad(self, x):
        return lax.psum_scatter(x.astype(BF16), "fsdp", scatter_dimension=0, tiled=True)

    def from_columns(self, x):
        return jnp.concatenate([t.astype(F32) for t in self.absolute(self.pieces(x))], axis=1)

    def from_rows(self, x):
        return jnp.concatenate(
            [t.astype(F32) for t in self.absolute(self.pieces(self.undeal(x)))], axis=0
        )


def local(
    ctx_size,
    fsdp_size,
    inputs,
    attn_norm,
    query_key_value_weight,
    w_out,
    mlp_norm,
    w_gate,
    w_up,
    w_down,
    cotangent,
    lengths,
    block_perm,
):
    comm = Comm(ctx_size, fsdp_size)
    own = inputs[0]
    count = own.shape[0]
    perm_row, len_row = block_perm[0], lengths[0]
    num_seqs = len_row.shape[0] - 1
    tokens = perm_row.shape[0] * BLOCK
    q_width, kv_width = QUERY_HEADS * HEAD_SIZE, KEY_VALUE_HEADS * HEAD_SIZE
    q_heads, kv_heads = QUERY_HEADS // ctx_size, KEY_VALUE_HEADS // ctx_size
    q_cols, kv_cols = q_heads * HEAD_SIZE, kv_heads * HEAD_SIZE

    order = jnp.arange(tokens, dtype=jnp.int32)
    rows = (comm.me ^ (order // count)) * count + order % count
    place, seg, inner = token_places(perm_row, len_row, rows)
    bias = mask_bias(place, seg, rows, num_seqs)
    cosine, sine = rope_tables(inner)

    wq_shard = jnp.concatenate(
        [
            comm.columns(query_key_value_weight[:, :q_width]),
            comm.columns(query_key_value_weight[:, q_width : q_width + kv_width]),
            comm.columns(query_key_value_weight[:, q_width + kv_width :]),
            attn_norm[:, None],
            mlp_norm[:, None],
        ],
        axis=1,
    )
    qkv_cols = q_cols + 2 * kv_cols
    wq_all = comm.weight(wq_shard)
    weight_qkv = wq_all[:, :qkv_cols]
    gain_one = wq_all[:, qkv_cols].astype(F32)
    gain_two = wq_all[:, qkv_cols + 1].astype(F32)
    weight_out = comm.weight(comm.deal(w_out))
    weight_gate = comm.weight(comm.columns(w_gate))
    weight_up = comm.weight(comm.columns(w_up))
    weight_down = comm.weight(comm.deal(w_down))

    x_all = comm.gather(own).astype(F32)
    hidden_one = (x_all * rms_scale(x_all) * gain_one).astype(BF16)
    projected = matmul(weight_qkv, hidden_one, 0, 1)
    q_t = rotate(projected[:q_cols].reshape(q_heads, HEAD_SIZE, tokens), cosine, sine).astype(BF16)
    k_t = rotate(
        projected[q_cols : q_cols + kv_cols].reshape(kv_heads, HEAD_SIZE, tokens), cosine, sine
    ).astype(BF16)
    v_t = projected[q_cols + kv_cols :].reshape(kv_heads, HEAD_SIZE, tokens).astype(BF16)
    key, value = k_t.transpose(0, 2, 1), v_t.transpose(0, 2, 1)
    attended, lse = attend(q_t, key, v_t, bias)
    merged = attended.reshape(q_cols, tokens)
    x_own = own.astype(F32)
    middle = x_own + comm.scatter(matmul(merged, weight_out, 0, 0))
    factor_two = rms_scale(middle)
    normed_two = middle * factor_two
    hidden_two = comm.gather((normed_two * gain_two).astype(BF16))
    gate = matmul(hidden_two, weight_gate, 1, 0)
    upper = matmul(hidden_two, weight_up, 1, 0)
    sigmoid = jax.nn.sigmoid(gate)
    activated = (gate * sigmoid * upper).astype(BF16)
    output = middle + comm.scatter(matmul(activated, weight_down, 1, 0))

    grad_low = comm.gather(cotangent[0])
    share_down = comm.grad(matmul(activated, grad_low, 0, 0))
    grad_act = matmul(grad_low, weight_down, 1, 1)
    grad_gate = (grad_act * upper * sigmoid * (1.0 + gate * (1.0 - sigmoid))).astype(BF16)
    grad_up = (grad_act * gate * sigmoid).astype(BF16)
    share_gate = comm.grad(matmul(hidden_two, grad_gate, 0, 0))
    share_up = comm.grad(matmul(hidden_two, grad_up, 0, 0))
    back = comm.scatter(
        matmul(grad_gate, weight_gate, 1, 1) + matmul(grad_up, weight_up, 1, 1)
    )
    gain_two_term = jnp.sum(back * normed_two, axis=0)
    grad_middle = cotangent[0].astype(F32) + rms_back(normed_two, factor_two, back * gain_two)
    grad_branch = comm.gather(grad_middle.astype(BF16))
    share_out = comm.grad(matmul(merged, grad_branch, 1, 0))
    grad_attended = matmul(weight_out, grad_branch, 1, 1).astype(BF16)
    dq, dk, dv = attend_back(
        q_t, key, k_t, value, bias, lse, grad_attended.reshape(q_heads, HEAD_SIZE, tokens)
    )
    grad_projected = jnp.concatenate(
        [
            rotate(dq, cosine, -sine).reshape(q_cols, tokens),
            rotate(dk, cosine, -sine).reshape(kv_cols, tokens),
            dv.reshape(kv_cols, tokens),
        ],
        axis=0,
    ).astype(BF16)
    grad_one = comm.scatter(matmul(grad_projected, weight_qkv, 0, 1))
    factor_one = rms_scale(x_own)
    normed_one = x_own * factor_one
    gain_one_term = jnp.sum(grad_one * normed_one, axis=0)
    grad_inputs = grad_middle + rms_back(normed_one, factor_one, grad_one * gain_one)
    term_qkv = jnp.concatenate(
        [
            matmul(hidden_one, grad_projected, 0, 1).astype(BF16),
            gain_one_term.astype(BF16)[:, None],
            gain_two_term.astype(BF16)[:, None],
        ],
        axis=1,
    )
    share_qkv = comm.grad(term_qkv)

    parts = [t.astype(F32) for t in comm.absolute(comm.pieces(share_qkv))]
    grad_qkv = jnp.concatenate(
        [t[:, :q_cols] for t in parts]
        + [t[:, q_cols : q_cols + kv_cols] for t in parts]
        + [t[:, q_cols + kv_cols : qkv_cols] for t in parts],
        axis=1,
    )
    gains = sum(t[:, qkv_cols:] for t in parts)
    return (
        output[None],
        grad_inputs[None],
        gains[:, 0],
        grad_qkv,
        comm.from_rows(share_out),
        gains[:, 1],
        comm.from_columns(share_gate),
        comm.from_columns(share_up),
        comm.from_rows(share_down),
    )


def solution(mesh):
    row = P("fsdp", None)
    tok = P("fsdp", "ctx", None)
    in_specs = (tok, P("fsdp"), row, row, P("fsdp"), row, row, row, tok, row, row)
    out_specs = (tok, tok, P("fsdp"), row, row, P("fsdp"), row, row, row)
    body = functools.partial(local, mesh.shape["ctx"], mesh.shape["fsdp"])
    return jax.shard_map(body, mesh=mesh, in_specs=in_specs, out_specs=out_specs, check_vma=False)
```
